32 devices in a mesh: grp: 8 (over z, x), mem: 4 (over y, core).
Axes of the slice: x: 2, y: 2, z: 4, core: 2. Of those that a mesh axis runs over, the one named last changes fastest.
Arguments:
- tokens: bfloat16 [8, 4096, 1152], P('grp', 'mem'), may hold values from -6 to 6
- attn_gain: bfloat16 [1152], P('mem'), may hold values from 0.5 to 1.5
- mlp_gain: bfloat16 [1152], P('mem'), may hold values from 0.5 to 1.5
- query_weight: bfloat16 [1152, 1152], P('grp', 'mem'), may hold values from -0.1875 to 0.1875
- key_matrix: bfloat16 [1152, 384], P('grp', 'mem'), may hold values from -0.1875 to 0.1875
- value_matrix: bfloat16 [1152, 384], P('grp', 'mem'), may hold values from -0.1875 to 0.1875
- output_weight: bfloat16 [1152, 1152], P('grp', 'mem'), may hold values from -4 to 4
- gate_weight: bfloat16 [1152, 3072], P('grp', 'mem'), may hold values from -0.1875 to 0.1875
- up_weight: bfloat16 [1152, 3072], P('grp', 'mem'), may hold values from -0.1875 to 0.1875
- down_weight: bfloat16 [3072, 1152], P('grp', 'mem'), may hold values from -0.109375 to 0.109375
- cotangent: bfloat16 [8, 4096, 1152], P('grp', 'mem'), may hold values from -6 to 6
Outputs:
- output: bfloat16 [8, 4096, 1152], P('grp', 'mem')
- tokens_grad: bfloat16 [8, 4096, 1152], P('grp', 'mem')
- attn_gain_grad: float32 [1152], P('mem')
- mlp_gain_grad: float32 [1152], P('mem')
- query_weight_grad: float32 [1152, 1152], P('grp', 'mem')
- key_weight_grad: float32 [1152, 384], P('grp', 'mem')
- value_weight_grad: float32 [1152, 384], P('grp', 'mem')
- output_weight_grad: float32 [1152, 1152], P('grp', 'mem')
- gate_weight_grad: float32 [1152, 3072], P('grp', 'mem')
- up_weight_grad: float32 [1152, 3072], P('grp', 'mem')
- down_weight_grad: float32 [3072, 1152], P('grp', 'mem')
The draws below stay inside these ranges and needn't reach their ends.
All inputs are finite; a program needn't handle non-finite values.
Results may differ from the reference program's by a relative error of at most 0.017.
Values may be sent and summed in bfloat16 or wider, within the bound.
No kernel may reach another device: no remote copies, remote signals or barrier semaphores. Data moves between devices by JAX's collectives and lax.ppermute only.
A program may use at most 384 MiB of HBM per device.

```python
import jax
import jax.numpy as jnp
from jax import lax

MODEL_WIDTH = 1152
QUERY_HEADS = 18
KEY_VALUE_HEADS = 6
HEAD_SIZE = 64
FF = 3072
PROMPT = 1024
CONT_LEN = 128
QUERY_BLOCK_ROWS = 512
GROUP_ROWS = 4096
N_GRP = 8
N_MEM = 4


def with_spikes(entries, rng, source, target, blocks, factor):
    owner, partner = [(jnp.arange(entries.shape[position]) // (entries.shape[position] // blocks)).reshape([-1 if axis == position else 1 for axis in range(entries.ndim)]) for position in (source, target)]
    chosen = jax.random.permutation(rng, blocks)[partner]
    strong = (owner == chosen) | (owner == (partner + blocks // 2) % blocks)
    return jnp.where(strong, factor * entries, entries)


def levels(rng, extent, split, low, high):
    def one(axis_at, blocks):
        draws = jax.random.uniform(jax.random.fold_in(jax.random.fold_in(rng, 6), axis_at), (blocks,), jnp.float32, low / len(split), high / len(split))
        return jnp.repeat(jnp.exp(draws), extent[axis_at] // blocks).reshape((-1,) + (1,) * (len(extent) - axis_at - 1))

    level = one(*split[0])
    for cut in split[1:]:
        level = level * one(*cut)
    return level


def scatter_about(own_key, dims, deviation, most, split=(), held_as=jnp.bfloat16):
    entries = deviation * jax.random.normal(own_key, dims, jnp.float32)
    if split:
        entries = entries * levels(own_key, dims, split, -0.22, 0.18)
    return jnp.clip(entries, -most, most).astype(held_as)


def heavy_noise(key, shape, scale, bound, pieces, heavy, kind=jnp.bfloat16):
    entries = scale * jax.random.normal(key, shape, jnp.float32)
    if pieces:
        entries = entries * levels(key, shape, pieces, -0.22, 0.18)
    return jnp.clip(with_spikes(entries, jax.random.fold_in(key, 3), *heavy), -bound, bound).astype(kind)


def setup_inputs(seed: int = 0) -> dict:
    key_list = jax.random.split(jax.random.key(seed), 12)
    tokens = scatter_about(key_list[0], (N_GRP, GROUP_ROWS, MODEL_WIDTH), 1.0, 6.0, ((0, 8), (1, 4)))
    attn_gain = jnp.clip(1.0 + 0.1 * jax.random.normal(key_list[1], (MODEL_WIDTH,), jnp.float32), 0.5, 1.5).astype(jnp.bfloat16)
    mlp_gain = jnp.clip(1.0 + 0.1 * jax.random.normal(key_list[2], (MODEL_WIDTH,), jnp.float32), 0.5, 1.5).astype(jnp.bfloat16)
    query_weight = scatter_about(key_list[3], (MODEL_WIDTH, QUERY_HEADS * HEAD_SIZE), MODEL_WIDTH ** -0.5, 0.1875, ((0, 8), (1, 4)))
    key_matrix = scatter_about(key_list[4], (MODEL_WIDTH, KEY_VALUE_HEADS * HEAD_SIZE), MODEL_WIDTH ** -0.5, 0.1875, ((0, 8), (1, 4)))
    value_matrix = scatter_about(key_list[5], (MODEL_WIDTH, KEY_VALUE_HEADS * HEAD_SIZE), MODEL_WIDTH ** -0.5, 0.1875, ((0, 8), (1, 4)))
    output_weight = scatter_about(key_list[6], (QUERY_HEADS * HEAD_SIZE, MODEL_WIDTH), 2 ** -0.5, 4.0, ((0, 8), (1, 4)))
    gate_weight = scatter_about(key_list[7], (MODEL_WIDTH, FF), MODEL_WIDTH ** -0.5, 0.1875, ((0, 8), (1, 4)))
    up_weight = scatter_about(key_list[8], (MODEL_WIDTH, FF), MODEL_WIDTH ** -0.5, 0.1875, ((0, 8), (1, 4)))
    down_weight = scatter_about(key_list[9], (FF, MODEL_WIDTH), FF ** -0.5, 0.109375, ((0, 8), (1, 4)))
    cotangent = heavy_noise(key_list[10], (N_GRP, GROUP_ROWS, MODEL_WIDTH), 1.0, 6.0, ((0, 8), (1, 4)), (1, 2, 4, 2.0))
    return dict(tokens=tokens, attn_gain=attn_gain, mlp_gain=mlp_gain, query_weight=query_weight, key_matrix=key_matrix, value_matrix=value_matrix, output_weight=output_weight, gate_weight=gate_weight, up_weight=up_weight, down_weight=down_weight, cotangent=cotangent)


HIGH = lax.Precision.HIGHEST
EPSILON = 1e-05

@jax.custom_vjp
def lower_precision(v):
    return lax.optimization_barrier(v.astype(jnp.bfloat16)).astype(jnp.float32)

@jax.custom_vjp
def lower_precision_back(v):
    return v

def low_keep(v):
    return (lower_precision(v), None)

def low_pass(kept, grad):
    return (grad,)

def back_keep(v):
    return (v, None)

def back_low(kept, grad):
    return (lower_precision(grad),)
lower_precision.defvjp(low_keep, low_pass)
lower_precision_back.defvjp(back_keep, back_low)

def matrix_product(left, right):
    return jnp.dot(left, right, precision=HIGH, preferred_element_type=jnp.float32)

def rms_norm(rows, gain):
    inverse = lax.rsqrt(lax.optimization_barrier(jnp.mean(rows * rows, axis=-1, keepdims=True)) + EPSILON)
    return rows * inverse * gain

def rotary_apply(rows, token_positions):
    half = HEAD_SIZE // 2
    freq = 10000.0 ** (-jnp.arange(half, dtype=jnp.float32) * 2.0 / HEAD_SIZE)
    angle = token_positions.astype(jnp.float32)[:, None] * freq[None, :]
    cosine_table = jnp.cos(angle)[:, None, :]
    sine_table = jnp.sin(angle)[:, None, :]
    first = rows[..., :half]
    second = rows[..., half:]
    return jnp.concatenate([first * cosine_table - second * sine_table, second * cosine_table + first * sine_table], axis=-1)

def attend(query_tile_block, key_rows_list, value_rows_list, allowed):
    row_count = query_tile_block.shape[0]
    grouped_heads = query_tile_block.reshape(row_count, KEY_VALUE_HEADS, QUERY_HEADS // KEY_VALUE_HEADS, HEAD_SIZE)
    scores = lower_precision_back(jnp.einsum('rhgd,lhd->hgrl', grouped_heads, key_rows_list, precision=HIGH) * HEAD_SIZE ** (-0.5))
    scores = jnp.where(allowed, scores, -1e+30)
    probs = jax.nn.softmax(scores, axis=-1)
    mixed_heads = jnp.einsum('hgrl,lhd->rhgd', lower_precision(probs), value_rows_list, precision=HIGH)
    return mixed_heads.reshape(row_count, QUERY_HEADS * HEAD_SIZE)

def prompt_attention(query_rows_list, key_rows_list, value_rows_list):
    block_list = query_rows_list.reshape(PROMPT // QUERY_BLOCK_ROWS, QUERY_BLOCK_ROWS, QUERY_HEADS, HEAD_SIZE)
    key_rows = jnp.arange(PROMPT)

    def single_block(item):
        index, query_tile_block = item
        query_rows = index * QUERY_BLOCK_ROWS + jnp.arange(QUERY_BLOCK_ROWS)
        allowed = key_rows[None, :] <= query_rows[:, None]
        return attend(query_tile_block, key_rows_list, value_rows_list, allowed)
    mixed_heads = lax.map(jax.checkpoint(single_block), (jnp.arange(PROMPT // QUERY_BLOCK_ROWS), block_list))
    return mixed_heads.reshape(PROMPT, QUERY_HEADS * HEAD_SIZE)

def continuation_attention(query_rows_list, key_rows_list, value_rows_list, prompt_key_rows, prompt_value_rows):
    block_list = PROMPT // QUERY_BLOCK_ROWS
    local = jnp.arange(QUERY_BLOCK_ROWS)
    own = (local[None, :] // CONT_LEN == local[:, None] // CONT_LEN) & (local[None, :] <= local[:, None])
    allowed = jnp.concatenate([jnp.ones((QUERY_BLOCK_ROWS, PROMPT), dtype=bool), own], axis=1)

    def single_block(item):
        query_tile_block, key_block, value_block = item
        all_keys = jnp.concatenate([prompt_key_rows, key_block], axis=0)
        all_values = jnp.concatenate([prompt_value_rows, value_block], axis=0)
        return attend(query_tile_block, all_keys, all_values, allowed)
    mixed_heads = lax.map(jax.checkpoint(single_block), (query_rows_list.reshape(block_list, QUERY_BLOCK_ROWS, QUERY_HEADS, HEAD_SIZE), key_rows_list.reshape(block_list, QUERY_BLOCK_ROWS, KEY_VALUE_HEADS, HEAD_SIZE), value_rows_list.reshape(block_list, QUERY_BLOCK_ROWS, KEY_VALUE_HEADS, HEAD_SIZE)))
    return mixed_heads.reshape(PROMPT, QUERY_HEADS * HEAD_SIZE)

def layer(rows, token_positions, attn_gain, mlp_gain, weights, attention):
    query_weight, key_matrix, value_matrix, output_weight, gate_weight, up_weight, down_weight = weights
    row_count = rows.shape[0]
    normalized_rows = lower_precision(rms_norm(rows, attn_gain))
    query_rows_list = lower_precision(rotary_apply(lower_precision_back(matrix_product(normalized_rows, query_weight)).reshape(row_count, QUERY_HEADS, HEAD_SIZE), token_positions))
    key_rows_list = lower_precision(rotary_apply(lower_precision_back(matrix_product(normalized_rows, key_matrix)).reshape(row_count, KEY_VALUE_HEADS, HEAD_SIZE), token_positions))
    value_rows_list = lower_precision(lower_precision_back(matrix_product(normalized_rows, value_matrix))).reshape(row_count, KEY_VALUE_HEADS, HEAD_SIZE)
    mixed_heads = lower_precision_back(lower_precision(attention(query_rows_list, key_rows_list, value_rows_list)))
    middle = rows + lower_precision_back(matrix_product(mixed_heads, output_weight))
    normed_two = lower_precision(rms_norm(middle, mlp_gain))
    gate = lower_precision_back(matrix_product(normed_two, gate_weight))
    up_values = lower_precision_back(matrix_product(normed_two, up_weight))
    hidden = lower_precision(jax.nn.silu(gate) * up_values)
    return (middle + matrix_product(hidden, down_weight), key_rows_list, value_rows_list)

def forward(rows_all, attn_gain, mlp_gain, weights):
    local = jnp.arange(PROMPT)
    holder_positions = PROMPT + local % CONT_LEN

    def group_rows(rows_group):
        width = rows_group.shape[1]
        first, prompt_key_rows, prompt_value_rows = layer(rows_group[:PROMPT], local, attn_gain, mlp_gain, weights, prompt_attention)

        def holder(rows_dev):

            def attention(query_rows_list, key_rows_list, value_rows_list):
                return continuation_attention(query_rows_list, key_rows_list, value_rows_list, prompt_key_rows, prompt_value_rows)
            result, unused_keys, unused_values = layer(rows_dev, holder_positions, attn_gain, mlp_gain, weights, attention)
            return result
        rest = lax.map(jax.checkpoint(holder), rows_group[PROMPT:].reshape(N_MEM - 1, PROMPT, width))
        return jnp.concatenate([first, rest.reshape(-1, width)], axis=0)
    return lax.map(jax.checkpoint(group_rows), rows_all)

def reference(tokens, attn_gain, mlp_gain, query_weight, key_matrix, value_matrix, output_weight, gate_weight, up_weight, down_weight, cotangent):
    weights = tuple((w.astype(jnp.float32) for w in (query_weight, key_matrix, value_matrix, output_weight, gate_weight, up_weight, down_weight)))
    result, pullback = jax.vjp(forward, tokens.astype(jnp.float32), attn_gain.astype(jnp.float32), mlp_gain.astype(jnp.float32), weights)
    tokens_grad, attn_grad, mlp_grad, weight_grads = pullback(cotangent.astype(jnp.float32))
    return (result.astype(jnp.bfloat16), tokens_grad.astype(jnp.bfloat16), attn_grad, mlp_grad, weight_grads[0], weight_grads[1], weight_grads[2], weight_grads[3], weight_grads[4], weight_grads[5], weight_grads[6])
```

```python
import functools

import jax
import jax.numpy as jnp
from jax import lax
from jax.experimental import pallas as pl
from jax.experimental.pallas import tpu as pltpu
from jax.sharding import PartitionSpec as P

QUERY_HEADS = 18
KEY_VALUE_HEADS = 6
HEAD_SIZE = 64
CONT_LEN = 128
EPSILON = 1e-05
NEG_FILL = -1e30
ROWS = 256
SCALE = HEAD_SIZE ** (-0.5)
F32 = jnp.float32
BF16 = jnp.bfloat16
VMEM_LIMIT = 56 * 2**20


def dot_nn(left, right):
    return lax.dot_general(left, right, (((1,), (0,)), ((), ())), preferred_element_type=F32)


def dot_nt(left, right):
    return lax.dot_general(left, right, (((1,), (1,)), ((), ())), preferred_element_type=F32)


def dot_tn(left, right):
    return lax.dot_general(left, right, (((0,), (0,)), ((), ())), preferred_element_type=F32)


def params(**more):
    return pltpu.CompilerParams(vmem_limit_bytes=VMEM_LIMIT, **more)


def turn(values, cosine, sine, direction):
    half = HEAD_SIZE // 2
    parts = []
    for head in range(values.shape[0] // HEAD_SIZE):
        first = values[head * HEAD_SIZE : head * HEAD_SIZE + half]
        second = values[head * HEAD_SIZE + half : (head + 1) * HEAD_SIZE]
        parts.append(first * cosine - direction * second * sine)
        parts.append(second * cosine + direction * first * sine)
    return jnp.concatenate(parts, axis=0)


def forward_kernel(flag_ref, q_ref, k_ref, v_ref, pk_ref, pv_ref, out_ref, lse_ref, kt_s, vt_s):
    step = pl.program_id(1)
    prompt = pk_ref.shape[0]

    @pl.when(step == 0)
    def _():
        for half in range(2):
            kt_s[half] = pk_ref[:, half * HEAD_SIZE : (half + 1) * HEAD_SIZE]
        vt_s[...] = pv_ref[...].T

    def heads(is_prompt):
        if is_prompt:
            key = lax.broadcasted_iota(jnp.int32, (prompt, ROWS), 0)
            row = lax.broadcasted_iota(jnp.int32, (prompt, ROWS), 1) + step * ROWS
            seen = key <= row
        else:
            key = lax.broadcasted_iota(jnp.int32, (ROWS, ROWS), 0)
            row = lax.broadcasted_iota(jnp.int32, (ROWS, ROWS), 1)
            seen = (key // CONT_LEN == row // CONT_LEN) & (key <= row)
            own_vt = v_ref[...].T
        per_pair = 2 * (QUERY_HEADS // KEY_VALUE_HEADS)
        outs = []
        for head in range(per_pair):
            kv = head // (per_pair // 2)
            span = slice(kv * HEAD_SIZE, (kv + 1) * HEAD_SIZE)
            q_t = q_ref[head * HEAD_SIZE : (head + 1) * HEAD_SIZE, :] * jnp.asarray(SCALE, BF16)
            scores = dot_nn(kt_s[kv], q_t)
            if is_prompt:
                scores = jnp.where(seen, scores, NEG_FILL)
                peak = jnp.max(scores, axis=0, keepdims=True)
                raised = jnp.exp(scores - peak)
                total = jnp.sum(raised, axis=0, keepdims=True)
                mixed = dot_nn(vt_s[span, :], raised.astype(BF16))
            else:
                own = jnp.where(seen, dot_nn(k_ref[:, span], q_t), NEG_FILL)
                peak = jnp.maximum(
                    jnp.max(scores, axis=0, keepdims=True), jnp.max(own, axis=0, keepdims=True)
                )
                raised = jnp.exp(scores - peak)
                own = jnp.exp(own - peak)
                total = jnp.sum(raised, axis=0, keepdims=True) + jnp.sum(
                    own, axis=0, keepdims=True
                )
                mixed = dot_nn(vt_s[span, :], raised.astype(BF16)) + dot_nn(
                    own_vt[span, :], own.astype(BF16)
                )
            outs.append(mixed / total)
            lse_ref[0, head : head + 1, :] = peak + jnp.log(total)
        out_ref[...] = jnp.concatenate(outs, axis=0).T.astype(BF16)

    @pl.when(flag_ref[0] == 1)
    def _():
        heads(True)

    @pl.when(flag_ref[0] == 0)
    def _():
        heads(False)


def attention_forward(flag, q_t, k, v, pk, pv):
    rows = k.shape[0]
    prompt = pk.shape[0]
    pairs = KEY_VALUE_HEADS // 2
    wide = q_t.shape[0] // pairs
    pair = 2 * HEAD_SIZE
    per_pair = wide // HEAD_SIZE
    return pl.pallas_call(
        forward_kernel,
        out_shape=(
            jax.ShapeDtypeStruct((rows, q_t.shape[0]), BF16),
            jax.ShapeDtypeStruct((pairs, 8, rows), F32),
        ),
        grid_spec=pltpu.PrefetchScalarGridSpec(
            num_scalar_prefetch=1,
            grid=(pairs, rows // ROWS),
            in_specs=[
                pl.BlockSpec((wide, ROWS), lambda p, i, f: (p, i)),
                pl.BlockSpec((ROWS, pair), lambda p, i, f: (i, p)),
                pl.BlockSpec((ROWS, pair), lambda p, i, f: (i, p)),
                pl.BlockSpec((prompt, pair), lambda p, i, f: (0, p)),
                pl.BlockSpec((prompt, pair), lambda p, i, f: (0, p)),
            ],
            out_specs=[
                pl.BlockSpec((ROWS, wide), lambda p, i, f: (i, p)),
                pl.BlockSpec((1, 8, ROWS), lambda p, i, f: (p, 0, i)),
            ],
            scratch_shapes=[
                pltpu.VMEM((2, prompt, HEAD_SIZE), BF16),
                pltpu.VMEM((pair, prompt), BF16),
            ],
        ),
        compiler_params=params(dimension_semantics=("arbitrary", "arbitrary")),
        name="attention_forward",
    )(flag, q_t, k, v, pk, pv)


def backward_kernel(
    flag_ref, q_ref, k_ref, v_ref, pk_ref, pv_ref, lse_ref, up_ref, mixed_ref, cos_ref, sin_ref,
    dq_ref, far_k_ref, far_v_ref, near_k_ref, near_v_ref, key_s, val_s, keyt_s,
):
    step = pl.program_id(1)
    prompt = pk_ref.shape[0]
    half_scale = jnp.asarray(SCALE, BF16)

    @pl.when(step == 0)
    def _():
        for half in range(2):
            key_s[half] = pk_ref[:, half * HEAD_SIZE : (half + 1) * HEAD_SIZE]
            val_s[half] = pv_ref[:, half * HEAD_SIZE : (half + 1) * HEAD_SIZE]
        keyt_s[...] = pk_ref[...].T * half_scale
        far_k_ref[...] = jnp.zeros_like(far_k_ref)
        far_v_ref[...] = jnp.zeros_like(far_v_ref)

    def heads(is_prompt):
        if is_prompt:
            key = lax.broadcasted_iota(jnp.int32, (prompt, ROWS), 0)
            row = lax.broadcasted_iota(jnp.int32, (prompt, ROWS), 1) + step * ROWS
            seen = key <= row
            near_k_ref[...] = jnp.zeros_like(near_k_ref)
            near_v_ref[...] = jnp.zeros_like(near_v_ref)
        else:
            key = lax.broadcasted_iota(jnp.int32, (ROWS, ROWS), 0)
            row = lax.broadcasted_iota(jnp.int32, (ROWS, ROWS), 1)
            seen = (key // CONT_LEN == row // CONT_LEN) & (key <= row)
            own_kt = k_ref[...].T * half_scale
        up = up_ref[...]
        up_t = up.T
        product_t = (up.astype(F32) * mixed_ref[...].astype(F32)).T
        per_pair = 2 * (QUERY_HEADS // KEY_VALUE_HEADS)
        turned = []
        far_k, far_v, near_k, near_v = [], [], [], []
        for kv in range(2):
            span = slice(kv * HEAD_SIZE, (kv + 1) * HEAD_SIZE)
            sums = None
            for inner in range(per_pair // 2):
                head = kv * (per_pair // 2) + inner
                place = slice(head * HEAD_SIZE, (head + 1) * HEAD_SIZE)
                q_t = q_ref[place, :] * half_scale
                q_n = q_t.T
                u_t = up_t[place, :]
                u_n = up[:, place]
                lse = lse_ref[0, head : head + 1, :]
                delta = jnp.sum(product_t[place, :], axis=0, keepdims=True)
                scores = dot_nn(key_s[kv], q_t)
                if is_prompt:
                    scores = jnp.where(seen, scores, NEG_FILL)
                probs = jnp.exp(scores - lse)
                grad = (probs * (dot_nn(val_s[kv], u_t) - delta)).astype(BF16)
                dq = dot_nn(keyt_s[span, :], grad)
                parts = [dot_nn(grad, q_n), dot_nn(probs.astype(BF16), u_n)]
                if not is_prompt:
                    own = jnp.where(seen, dot_nn(k_ref[:, span], q_t), NEG_FILL)
                    own = jnp.exp(own - lse)
                    own_grad = (own * (dot_nn(v_ref[:, span], u_t) - delta)).astype(BF16)
                    dq = dq + dot_nn(own_kt[span, :], own_grad)
                    parts += [dot_nn(own_grad, q_n), dot_nn(own.astype(BF16), u_n)]
                turned.append(dq)
                sums = parts if sums is None else [a + b for a, b in zip(sums, parts)]
            far_k.append(sums[0])
            far_v.append(sums[1])
            if not is_prompt:
                near_k.append(sums[2])
                near_v.append(sums[3])
        dq_ref[...] = (
            turn(jnp.concatenate(turned, axis=0), cos_ref[...], sin_ref[...], -1.0)
            .T.astype(BF16)
        )
        far_k_ref[...] += jnp.concatenate(far_k, axis=1)
        far_v_ref[...] += jnp.concatenate(far_v, axis=1)
        if not is_prompt:
            near_k_ref[...] = jnp.concatenate(near_k, axis=1)
            near_v_ref[...] = jnp.concatenate(near_v, axis=1)

    @pl.when(flag_ref[0] == 1)
    def _():
        heads(True)

    @pl.when(flag_ref[0] == 0)
    def _():
        heads(False)


def attention_backward(flag, q_t, k, v, pk, pv, lse, up, mixed, cosine, sine):
    rows = k.shape[0]
    prompt = pk.shape[0]
    pairs = KEY_VALUE_HEADS // 2
    wide = q_t.shape[0] // pairs
    pair = 2 * HEAD_SIZE
    near = pl.BlockSpec((ROWS, pair), lambda p, i, f: (i, p))
    far = pl.BlockSpec((prompt, pair), lambda p, i, f: (0, p))
    band = pl.BlockSpec((ROWS, wide), lambda p, i, f: (i, p))
    table = pl.BlockSpec((HEAD_SIZE // 2, ROWS), lambda p, i, f: (0, i))
    return pl.pallas_call(
        backward_kernel,
        out_shape=(
            jax.ShapeDtypeStruct((rows, q_t.shape[0]), BF16),
            jax.ShapeDtypeStruct(pk.shape, F32),
            jax.ShapeDtypeStruct(pv.shape, F32),
            jax.ShapeDtypeStruct(k.shape, F32),
            jax.ShapeDtypeStruct(v.shape, F32),
        ),
        grid_spec=pltpu.PrefetchScalarGridSpec(
            num_scalar_prefetch=1,
            grid=(pairs, rows // ROWS),
            in_specs=[
                pl.BlockSpec((wide, ROWS), lambda p, i, f: (p, i)),
                near, near, far, far,
                pl.BlockSpec((1, 8, ROWS), lambda p, i, f: (p, 0, i)),
                band, band, table, table,
            ],
            out_specs=[band, far, far, near, near],
            scratch_shapes=[
                pltpu.VMEM((2, prompt, HEAD_SIZE), BF16),
                pltpu.VMEM((2, prompt, HEAD_SIZE), BF16),
                pltpu.VMEM((pair, prompt), BF16),
            ],
        ),
        compiler_params=params(dimension_semantics=("arbitrary", "arbitrary")),
        name="attention_backward",
    )(flag, q_t, k, v, pk, pv, lse, up, mixed, cosine, sine)


def project_kernel(x_ref, gain_ref, w_ref, cos_ref, sin_ref, normed_ref, q_ref, k_ref, v_ref):
    x = x_ref[...].astype(F32)
    inverse = lax.rsqrt(jnp.mean(x * x, axis=-1, keepdims=True) + EPSILON)
    normed = (x * inverse * gain_ref[...].astype(F32)).astype(BF16)
    normed_ref[...] = normed
    members = w_ref.shape[0]
    kw = k_ref.shape[1] // members
    keys, values, queries = [], [], []
    for member in range(members):
        piece = dot_nn(normed, w_ref[member]).T
        keys.append(piece[:kw])
        values.append(piece[kw : 2 * kw])
        queries.append(piece[2 * kw :])
    cosine, sine = cos_ref[...], sin_ref[...]
    q_ref[...] = turn(jnp.concatenate(queries, axis=0), cosine, sine, 1.0).astype(BF16)
    k_ref[...] = turn(jnp.concatenate(keys, axis=0), cosine, sine, 1.0).T.astype(BF16)
    v_ref[...] = jnp.concatenate(values, axis=0).T.astype(BF16)


def project(x, gain, w, cosine, sine):
    rows, width = x.shape
    members = w.shape[0]
    qw = QUERY_HEADS * HEAD_SIZE
    kw = KEY_VALUE_HEADS * HEAD_SIZE
    band = pl.BlockSpec((ROWS, width), lambda i: (i, 0))
    table = pl.BlockSpec((HEAD_SIZE // 2, ROWS), lambda i: (0, i))
    thin = pl.BlockSpec((ROWS, kw), lambda i: (i, 0))
    return pl.pallas_call(
        project_kernel,
        out_shape=(
            jax.ShapeDtypeStruct((rows, width), BF16),
            jax.ShapeDtypeStruct((qw, rows), BF16),
            jax.ShapeDtypeStruct((rows, kw), BF16),
            jax.ShapeDtypeStruct((rows, kw), BF16),
        ),
        grid=(rows // ROWS,),
        in_specs=[
            band,
            pl.BlockSpec((1, width), lambda i: (0, 0)),
            pl.BlockSpec(w.shape, lambda i: (0, 0, 0), pipeline_mode=pl.Buffered(1)),
            table,
            table,
        ],
        out_specs=[band, pl.BlockSpec((qw, ROWS), lambda i: (0, i)), thin, thin],
        compiler_params=params(dimension_semantics=("arbitrary",)),
        name="project",
    )(x, gain, w, cosine, sine)


def finish_kernel(
    flag_ref, x_ref, gain_ref, w_ref, cos_ref, sin_ref, mid_ref, qraw_ref, far_ref, nk_ref, nv_ref,
    tokens_ref, gain_grad_ref, raw_ref,
):
    kw = nk_ref.shape[1]
    members = w_ref.shape[0]
    prompt = flag_ref[0] == 1
    far = far_ref[...].astype(F32)
    key_sum = jnp.where(prompt, far[:, :kw], nk_ref[...])
    value_raw = jnp.where(prompt, far[:, kw:], nv_ref[...]).astype(BF16)
    key_raw = turn(key_sum.T, cos_ref[...], sin_ref[...], -1.0).T.astype(BF16)
    query_raw = qraw_ref[...]
    ks = kw // members
    qs = query_raw.shape[1] // members
    normed_grad = None
    for member in range(members):
        raw = jnp.concatenate(
            [
                key_raw[:, member * ks : (member + 1) * ks],
                value_raw[:, member * ks : (member + 1) * ks],
                query_raw[:, member * qs : (member + 1) * qs],
            ],
            axis=1,
        )
        raw_ref[member] = raw
        part = dot_nt(raw, w_ref[member])
        normed_grad = part if normed_grad is None else normed_grad + part
    x = x_ref[...].astype(F32)
    width = x.shape[1]
    inverse = lax.rsqrt(jnp.mean(x * x, axis=-1, keepdims=True) + EPSILON)
    scaled = normed_grad * gain_ref[...].astype(F32)
    inner = jnp.sum(scaled * x, axis=-1, keepdims=True)
    rows_grad = scaled * inverse - x * (inverse**3 * inner / width)
    tokens_ref[...] = (mid_ref[...] + rows_grad).astype(BF16)

    @pl.when(pl.program_id(0) == 0)
    def _():
        gain_grad_ref[...] = jnp.zeros_like(gain_grad_ref)

    gain_grad_ref[...] += jnp.sum(normed_grad * x * inverse, axis=0, keepdims=True)


def finish(flag, x, gain, w, cosine, sine, middle_grad, query_raw, far, near_k, near_v):
    rows, width = x.shape
    kw = near_k.shape[1]
    band = pl.BlockSpec((ROWS, width), lambda i, f: (i, 0))
    row = pl.BlockSpec((1, width), lambda i, f: (0, 0))
    table = pl.BlockSpec((HEAD_SIZE // 2, ROWS), lambda i, f: (0, i))
    thin = pl.BlockSpec((ROWS, kw), lambda i, f: (i, 0))
    return pl.pallas_call(
        finish_kernel,
        out_shape=(
            jax.ShapeDtypeStruct((rows, width), BF16),
            jax.ShapeDtypeStruct((1, width), F32),
            jax.ShapeDtypeStruct((w.shape[0], rows, w.shape[2]), BF16),
        ),
        grid_spec=pltpu.PrefetchScalarGridSpec(
            num_scalar_prefetch=1,
            grid=(rows // ROWS,),
            in_specs=[
                band,
                row,
                pl.BlockSpec(w.shape, lambda i, f: (0, 0, 0), pipeline_mode=pl.Buffered(1)),
                table,
                table,
                band,
                pl.BlockSpec((ROWS, query_raw.shape[1]), lambda i, f: (i, 0)),
                pl.BlockSpec((ROWS, 2 * kw), lambda i, f: (i, 0)),
                thin,
                thin,
            ],
            out_specs=[
                band,
                row,
                pl.BlockSpec((w.shape[0], ROWS, w.shape[2]), lambda i, f: (0, i, 0)),
            ],
        ),
        compiler_params=params(dimension_semantics=("arbitrary",)),
        name="finish",
    )(flag, x, gain, w, cosine, sine, middle_grad, query_raw, far, near_k, near_v)


def spread_down(value, axis):
    size = lax.axis_size(axis)
    index = lax.axis_index(axis)
    bit = size // 2
    while bit >= 1:
        pairs = [(i, i + bit) for i in range(0, size, 2 * bit)]
        received = lax.ppermute(value, axis, pairs)
        value = jnp.where(index % (2 * bit) == bit, received, value)
        bit //= 2
    return value


def sum_up(value, axis):
    size = lax.axis_size(axis)
    bit = 1
    while bit < size:
        pairs = [(i + bit, i) for i in range(0, size, 2 * bit)]
        received = lax.ppermute(value, axis, pairs)
        value = (value.astype(F32) + received.astype(F32)).astype(value.dtype)
        bit *= 2
    return value


def assemble(piece, groups, members):
    height, width = piece.shape[1:]
    return (
        piece.reshape(groups, members, height, width)
        .transpose(0, 2, 1, 3)
        .reshape(groups * height, members * width)
    )


def disperse(full, groups, members):
    height = full.shape[0] // groups
    width = full.shape[1] // members
    return (
        full.reshape(groups, height, members, width)
        .transpose(0, 2, 1, 3)
        .reshape(groups * members, height, width)
    )


def gather(shard):
    return lax.all_gather(shard[None], ("grp", "mem"), axis=0, tiled=True)


def scatter(terms):
    return lax.psum_scatter(terms, ("grp", "mem"), scatter_dimension=0, tiled=True)[0].astype(F32)


def body(
    tokens, attn_gain, mlp_gain, query_weight, key_matrix, value_matrix, output_weight,
    gate_weight, up_weight, down_weight, cotangent,
):
    groups = lax.axis_size("grp")
    members = lax.axis_size("mem")
    qs = query_weight.shape[1]
    ks = key_matrix.shape[1]
    fs = gate_weight.shape[1]
    height = query_weight.shape[0]
    narrow = 2 * ks + qs
    gains = jnp.pad(jnp.stack([attn_gain, mlp_gain]), ((0, 6), (0, narrow - attn_gain.shape[0])))
    first = jnp.concatenate(
        [jnp.concatenate([key_matrix, value_matrix, query_weight], axis=1), gains], axis=0
    )
    first = gather(first)
    second = gather(output_weight)
    third = gather(jnp.concatenate([gate_weight, up_weight], axis=1))
    fourth = gather(down_weight)
    gain_rows = first[:members, height : height + 2, : attn_gain.shape[0]]
    gain_one = gain_rows[:, 0].reshape(1, -1)
    gain_two = gain_rows[:, 1].reshape(1, -1)
    w_qkv = (
        first[:, :height]
        .reshape(groups, members, height, narrow)
        .transpose(1, 0, 2, 3)
        .reshape(members, groups * height, narrow)
    )
    prompt_flag = lax.axis_index("mem") == 0
    flag = prompt_flag.astype(jnp.int32).reshape(1)
    x = tokens[0]
    rows = x.shape[0]
    local = jnp.arange(rows)
    positions = jnp.where(prompt_flag, local, rows + local % CONT_LEN).astype(F32)
    half = HEAD_SIZE // 2
    freq = 10000.0 ** (-jnp.arange(half, dtype=F32) * 2.0 / HEAD_SIZE)
    angle = freq[:, None] * positions[None, :]
    cosine, sine = jnp.cos(angle), jnp.sin(angle)
    normed, q_t, k, v = project(x, gain_one, w_qkv, cosine, sine)
    kw = k.shape[1]
    common = spread_down(jnp.concatenate([k, v], axis=1), "mem")
    pk, pv = common[:, :kw], common[:, kw:]
    mixed, lse = attention_forward(flag, q_t, k, v, pk, pv)
    w_out = assemble(second, groups, members)
    w_gate = assemble(third[:, :, :fs], groups, members)
    w_up = assemble(third[:, :, fs:], groups, members)
    w_down = assemble(fourth, groups, members)
    middle = x.astype(F32) + dot_nn(mixed, w_out)
    inverse_two = lax.rsqrt(jnp.mean(middle * middle, axis=-1, keepdims=True) + EPSILON)
    gain_two = gain_two.astype(F32)
    normed_two = (middle * inverse_two * gain_two).astype(BF16)
    gate = dot_nn(normed_two, w_gate)
    up = dot_nn(normed_two, w_up)
    sigma = jax.nn.sigmoid(gate)
    hidden = (gate * sigma * up).astype(BF16)
    output = (middle + dot_nn(hidden, w_down)).astype(BF16)[None]
    upstream = cotangent[0]
    down_grad = scatter(disperse(dot_tn(hidden, upstream).astype(BF16), groups, members))
    hidden_grad = dot_nt(upstream, w_down)
    gate_grad = (hidden_grad * up * sigma * (1.0 + gate * (1.0 - sigma))).astype(BF16)
    up_grad = (hidden_grad * gate * sigma).astype(BF16)
    pair_grad = scatter(
        jnp.concatenate(
            [
                disperse(dot_tn(normed_two, gate_grad).astype(BF16), groups, members),
                disperse(dot_tn(normed_two, up_grad).astype(BF16), groups, members),
            ],
            axis=2,
        )
    )
    normed_two_grad = dot_nt(gate_grad, w_gate) + dot_nt(up_grad, w_up)
    scaled = normed_two_grad * gain_two
    mlp_gain_grad = jnp.sum(normed_two_grad * middle * inverse_two, axis=0)
    inner = jnp.sum(scaled * middle, axis=-1, keepdims=True)
    middle_grad = (
        upstream.astype(F32)
        + scaled * inverse_two
        - middle * (inverse_two**3 * inner / middle.shape[-1])
    )
    middle_low = middle_grad.astype(BF16)
    mixed_grad = dot_nt(middle_low, w_out).astype(BF16)
    query_raw, far_k, far_v, near_k, near_v = attention_backward(
        flag, q_t, k, v, pk, pv, lse, mixed_grad, mixed, cosine, sine
    )
    far = sum_up(jnp.concatenate([far_k, far_v], axis=1).astype(BF16), "mem")
    tokens_grad, attn_gain_grad, raw = finish(
        flag, x, gain_one, w_qkv, cosine, sine, middle_grad, query_raw, far, near_k, near_v
    )
    out_terms = disperse(dot_tn(mixed, middle_low).astype(BF16), groups, members)
    qkv_terms = jnp.stack(
        [
            dot_tn(normed, raw[member]).astype(BF16).reshape(groups, height, narrow)
            for member in range(members)
        ],
        axis=1,
    ).reshape(groups * members, height, narrow)
    gain_terms = jnp.stack([attn_gain_grad[0], mlp_gain_grad]).astype(BF16)
    gain_terms = gain_terms.reshape(2, members, -1).transpose(1, 0, 2)
    gain_terms = jnp.pad(
        jnp.tile(gain_terms, (groups, 1, 1)), ((0, 0), (0, 6), (0, narrow - gain_terms.shape[2]))
    )
    last = scatter(
        jnp.concatenate(
            [
                jnp.concatenate([qkv_terms, gain_terms], axis=1),
                jnp.pad(out_terms, ((0, 0), (0, 8), (0, 0))),
            ],
            axis=2,
        )
    )
    gs = attn_gain.shape[0]
    return (
        output,
        tokens_grad[None],
        last[height, :gs],
        last[height + 1, :gs],
        last[:height, 2 * ks : narrow],
        last[:height, :ks],
        last[:height, ks : 2 * ks],
        last[:height, narrow:],
        pair_grad[:, :fs],
        pair_grad[:, fs:],
        down_grad,
    )


def solution(mesh):
    rows = P("grp", "mem", None)
    both = P("grp", "mem")
    gain = P("mem")
    return jax.shard_map(
        body,
        mesh=mesh,
        in_specs=(rows, gain, gain) + (both,) * 7 + (rows,),
        out_specs=(rows, rows, gain, gain) + (both,) * 7,
        check_vma=False,
    )
```

```python
import functools

import jax
import jax.numpy as jnp
from jax import lax
from jax.experimental import pallas as pl
from jax.experimental.pallas import tpu as pltpu
from jax.sharding import PartitionSpec as P

QUERY_HEADS = 18
KEY_VALUE_HEADS = 6
HEAD_SIZE = 64
CONT_LEN = 128
EPSILON = 1e-05
NEG_FILL = -1e30
ROWS = 256
SCALE = HEAD_SIZE ** (-0.5)
F32 = jnp.float32
BF16 = jnp.bfloat16
VMEM_LIMIT = 56 * 2**20


def dot_nn(left, right):
    return lax.dot_general(left, right, (((1,), (0,)), ((), ())), preferred_element_type=F32)


def dot_nt(left, right):
    return lax.dot_general(left, right, (((1,), (1,)), ((), ())), preferred_element_type=F32)


def dot_tn(left, right):
    return lax.dot_general(left, right, (((0,), (0,)), ((), ())), preferred_element_type=F32)


def params(**more):
    return pltpu.CompilerParams(vmem_limit_bytes=VMEM_LIMIT, **more)


def turn(values, cosine, sine, direction):
    half = HEAD_SIZE // 2
    parts = []
    for head in range(values.shape[0] // HEAD_SIZE):
        first = values[head * HEAD_SIZE : head * HEAD_SIZE + half]
        second = values[head * HEAD_SIZE + half : (head + 1) * HEAD_SIZE]
        parts.append(first * cosine - direction * second * sine)
        parts.append(second * cosine + direction * first * sine)
    return jnp.concatenate(parts, axis=0)


def forward_kernel(flag_ref, q_ref, k_ref, v_ref, pk_ref, pv_ref, out_ref, lse_ref, kt_s, vt_s):
    step = pl.program_id(1)
    prompt = pk_ref.shape[0]

    @pl.when(step == 0)
    def _():
        for half in range(2):
            kt_s[half] = pk_ref[:, half * HEAD_SIZE : (half + 1) * HEAD_SIZE]
        vt_s[...] = pv_ref[...].T

    def heads(is_prompt):
        if is_prompt:
            key = lax.broadcasted_iota(jnp.int32, (prompt, ROWS), 0)
            row = lax.broadcasted_iota(jnp.int32, (prompt, ROWS), 1) + step * ROWS
            seen = key <= row
        else:
            key = lax.broadcasted_iota(jnp.int32, (ROWS, ROWS), 0)
            row = lax.broadcasted_iota(jnp.int32, (ROWS, ROWS), 1)
            seen = (key // CONT_LEN == row // CONT_LEN) & (key <= row)
            own_vt = v_ref[...].T
        per_pair = 2 * (QUERY_HEADS // KEY_VALUE_HEADS)
        outs = []
        for head in range(per_pair):
            kv = head // (per_pair // 2)
            span = slice(kv * HEAD_SIZE, (kv + 1) * HEAD_SIZE)
            q_t = q_ref[head * HEAD_SIZE : (head + 1) * HEAD_SIZE, :] * jnp.asarray(SCALE, BF16)
            scores = dot_nn(kt_s[kv], q_t)
            if is_prompt:
                scores = jnp.where(seen, scores, NEG_FILL)
                peak = jnp.max(scores, axis=0, keepdims=True)
                raised = jnp.exp(scores - peak)
                total = jnp.sum(raised, axis=0, keepdims=True)
                mixed = dot_nn(vt_s[span, :], raised.astype(BF16))
            else:
                own = jnp.where(seen, dot_nn(k_ref[:, span], q_t), NEG_FILL)
                peak = jnp.maximum(
                    jnp.max(scores, axis=0, keepdims=True), jnp.max(own, axis=0, keepdims=True)
                )
                raised = jnp.exp(scores - peak)
                own = jnp.exp(own - peak)
                total = jnp.sum(raised, axis=0, keepdims=True) + jnp.sum(
                    own, axis=0, keepdims=True
                )
                mixed = dot_nn(vt_s[span, :], raised.astype(BF16)) + dot_nn(
                    own_vt[span, :], own.astype(BF16)
                )
            outs.append(mixed / total)
            lse_ref[0, head : head + 1, :] = peak + jnp.log(total)
        out_ref[...] = jnp.concatenate(outs, axis=0).T.astype(BF16)

    @pl.when(flag_ref[0] == 1)
    def _():
        heads(True)

    @pl.when(flag_ref[0] == 0)
    def _():
        heads(False)


def attention_forward(flag, q_t, k, v, pk, pv):
    rows = k.shape[0]
    prompt = pk.shape[0]
    pairs = KEY_VALUE_HEADS // 2
    wide = q_t.shape[0] // pairs
    pair = 2 * HEAD_SIZE
    per_pair = wide // HEAD_SIZE
    return pl.pallas_call(
        forward_kernel,
        out_shape=(
            jax.ShapeDtypeStruct((rows, q_t.shape[0]), BF16),
            jax.ShapeDtypeStruct((pairs, 8, rows), F32),
        ),
        grid_spec=pltpu.PrefetchScalarGridSpec(
            num_scalar_prefetch=1,
            grid=(pairs, rows // ROWS),
            in_specs=[
                pl.BlockSpec((wide, ROWS), lambda p, i, f: (p, i)),
                pl.BlockSpec((ROWS, pair), lambda p, i, f: (i, p)),
                pl.BlockSpec((ROWS, pair), lambda p, i, f: (i, p)),
                pl.BlockSpec((prompt, pair), lambda p, i, f: (0, p)),
                pl.BlockSpec((prompt, pair), lambda p, i, f: (0, p)),
            ],
            out_specs=[
                pl.BlockSpec((ROWS, wide), lambda p, i, f: (i, p)),
                pl.BlockSpec((1, 8, ROWS), lambda p, i, f: (p, 0, i)),
            ],
            scratch_shapes=[
                pltpu.VMEM((2, prompt, HEAD_SIZE), BF16),
                pltpu.VMEM((pair, prompt), BF16),
            ],
        ),
        compiler_params=params(dimension_semantics=("arbitrary", "arbitrary")),
        name="attention_forward",
    )(flag, q_t, k, v, pk, pv)


def backward_kernel(
    flag_ref, q_ref, k_ref, v_ref, pk_ref, pv_ref, lse_ref, up_ref, mixed_ref, cos_ref, sin_ref,
    dq_ref, far_k_ref, far_v_ref, near_k_ref, near_v_ref, key_s, val_s, keyt_s,
):
    step = pl.program_id(1)
    prompt = pk_ref.shape[0]
    half_scale = jnp.asarray(SCALE, BF16)

    @pl.when(step == 0)
    def _():
        for half in range(2):
            key_s[half] = pk_ref[:, half * HEAD_SIZE : (half + 1) * HEAD_SIZE]
            val_s[half] = pv_ref[:, half * HEAD_SIZE : (half + 1) * HEAD_SIZE]
        keyt_s[...] = pk_ref[...].T * half_scale
        far_k_ref[...] = jnp.zeros_like(far_k_ref)
        far_v_ref[...] = jnp.zeros_like(far_v_ref)

    def heads(is_prompt):
        if is_prompt:
            key = lax.broadcasted_iota(jnp.int32, (prompt, ROWS), 0)
            row = lax.broadcasted_iota(jnp.int32, (prompt, ROWS), 1) + step * ROWS
            seen = key <= row
            near_k_ref[...] = jnp.zeros_like(near_k_ref)
            near_v_ref[...] = jnp.zeros_like(near_v_ref)
        else:
            key = lax.broadcasted_iota(jnp.int32, (ROWS, ROWS), 0)
            row = lax.broadcasted_iota(jnp.int32, (ROWS, ROWS), 1)
            seen = (key // CONT_LEN == row // CONT_LEN) & (key <= row)
            own_kt = k_ref[...].T * half_scale
        up = up_ref[...]
        up_t = up.T
        product_t = (up.astype(F32) * mixed_ref[...].astype(F32)).T
        per_pair = 2 * (QUERY_HEADS // KEY_VALUE_HEADS)
        turned = []
        far_k, far_v, near_k, near_v = [], [], [], []
        for kv in range(2):
            span = slice(kv * HEAD_SIZE, (kv + 1) * HEAD_SIZE)
            sums = None
            for inner in range(per_pair // 2):
                head = kv * (per_pair // 2) + inner
                place = slice(head * HEAD_SIZE, (head + 1) * HEAD_SIZE)
                q_t = q_ref[place, :] * half_scale
                q_n = q_t.T
                u_t = up_t[place, :]
                u_n = up[:, place]
                lse = lse_ref[0, head : head + 1, :]
                delta = jnp.sum(product_t[place, :], axis=0, keepdims=True)
                scores = dot_nn(key_s[kv], q_t)
                if is_prompt:
                    scores = jnp.where(seen, scores, NEG_FILL)
                probs = jnp.exp(scores - lse)
                grad = (probs * (dot_nn(val_s[kv], u_t) - delta)).astype(BF16)
                dq = dot_nn(keyt_s[span, :], grad)
                parts = [dot_nn(grad, q_n), dot_nn(probs.astype(BF16), u_n)]
                if not is_prompt:
                    own = jnp.where(seen, dot_nn(k_ref[:, span], q_t), NEG_FILL)
                    own = jnp.exp(own - lse)
                    own_grad = (own * (dot_nn(v_ref[:, span], u_t) - delta)).astype(BF16)
                    dq = dq + dot_nn(own_kt[span, :], own_grad)
                    parts += [dot_nn(own_grad, q_n), dot_nn(own.astype(BF16), u_n)]
                turned.append(dq)
                sums = parts if sums is None else [a + b for a, b in zip(sums, parts)]
            far_k.append(sums[0])
            far_v.append(sums[1])
            if not is_prompt:
                near_k.append(sums[2])
                near_v.append(sums[3])
        dq_ref[...] = (
            turn(jnp.concatenate(turned, axis=0), cos_ref[...], sin_ref[...], -1.0)
            .T.astype(BF16)
        )
        far_k_ref[...] += jnp.concatenate(far_k, axis=1)
        far_v_ref[...] += jnp.concatenate(far_v, axis=1)
        if not is_prompt:
            near_k_ref[...] = jnp.concatenate(near_k, axis=1)
            near_v_ref[...] = jnp.concatenate(near_v, axis=1)

    @pl.when(flag_ref[0] == 1)
    def _():
        heads(True)

    @pl.when(flag_ref[0] == 0)
    def _():
        heads(False)


def attention_backward(flag, q_t, k, v, pk, pv, lse, up, mixed, cosine, sine):
    rows = k.shape[0]
    prompt = pk.shape[0]
    pairs = KEY_VALUE_HEADS // 2
    wide = q_t.shape[0] // pairs
    pair = 2 * HEAD_SIZE
    near = pl.BlockSpec((ROWS, pair), lambda p, i, f: (i, p))
    far = pl.BlockSpec((prompt, pair), lambda p, i, f: (0, p))
    band = pl.BlockSpec((ROWS, wide), lambda p, i, f: (i, p))
    table = pl.BlockSpec((HEAD_SIZE // 2, ROWS), lambda p, i, f: (0, i))
    return pl.pallas_call(
        backward_kernel,
        out_shape=(
            jax.ShapeDtypeStruct((rows, q_t.shape[0]), BF16),
            jax.ShapeDtypeStruct(pk.shape, F32),
            jax.ShapeDtypeStruct(pv.shape, F32),
            jax.ShapeDtypeStruct(k.shape, F32),
            jax.ShapeDtypeStruct(v.shape, F32),
        ),
        grid_spec=pltpu.PrefetchScalarGridSpec(
            num_scalar_prefetch=1,
            grid=(pairs, rows // ROWS),
            in_specs=[
                pl.BlockSpec((wide, ROWS), lambda p, i, f: (p, i)),
                near, near, far, far,
                pl.BlockSpec((1, 8, ROWS), lambda p, i, f: (p, 0, i)),
                band, band, table, table,
            ],
            out_specs=[band, far, far, near, near],
            scratch_shapes=[
                pltpu.VMEM((2, prompt, HEAD_SIZE), BF16),
                pltpu.VMEM((2, prompt, HEAD_SIZE), BF16),
                pltpu.VMEM((pair, prompt), BF16),
            ],
        ),
        compiler_params=params(dimension_semantics=("arbitrary", "arbitrary")),
        name="attention_backward",
    )(flag, q_t, k, v, pk, pv, lse, up, mixed, cosine, sine)


def project_kernel(x_ref, gain_ref, w_ref, cos_ref, sin_ref, normed_ref, q_ref, k_ref, v_ref):
    x = x_ref[...].astype(F32)
    inverse = lax.rsqrt(jnp.mean(x * x, axis=-1, keepdims=True) + EPSILON)
    normed = (x * inverse * gain_ref[...].astype(F32)).astype(BF16)
    normed_ref[...] = normed
    members = w_ref.shape[0]
    kw = k_ref.shape[1] // members
    keys, values, queries = [], [], []
    for member in range(members):
        piece = dot_nn(normed, w_ref[member]).T
        keys.append(piece[:kw])
        values.append(piece[kw : 2 * kw])
        queries.append(piece[2 * kw :])
    cosine, sine = cos_ref[...], sin_ref[...]
    q_ref[...] = turn(jnp.concatenate(queries, axis=0), cosine, sine, 1.0).astype(BF16)
    k_ref[...] = turn(jnp.concatenate(keys, axis=0), cosine, sine, 1.0).T.astype(BF16)
    v_ref[...] = jnp.concatenate(values, axis=0).T.astype(BF16)


def project(x, gain, w, cosine, sine):
    rows, width = x.shape
    members = w.shape[0]
    qw = QUERY_HEADS * HEAD_SIZE
    kw = KEY_VALUE_HEADS * HEAD_SIZE
    band = pl.BlockSpec((ROWS, width), lambda i: (i, 0))
    table = pl.BlockSpec((HEAD_SIZE // 2, ROWS), lambda i: (0, i))
    thin = pl.BlockSpec((ROWS, kw), lambda i: (i, 0))
    return pl.pallas_call(
        project_kernel,
        out_shape=(
            jax.ShapeDtypeStruct((rows, width), BF16),
            jax.ShapeDtypeStruct((qw, rows), BF16),
            jax.ShapeDtypeStruct((rows, kw), BF16),
            jax.ShapeDtypeStruct((rows, kw), BF16),
        ),
        grid=(rows // ROWS,),
        in_specs=[
            band,
            pl.BlockSpec((1, width), lambda i: (0, 0)),
            pl.BlockSpec(w.shape, lambda i: (0, 0, 0), pipeline_mode=pl.Buffered(1)),
            table,
            table,
        ],
        out_specs=[band, pl.BlockSpec((qw, ROWS), lambda i: (0, i)), thin, thin],
        compiler_params=params(dimension_semantics=("arbitrary",)),
        name="project",
    )(x, gain, w, cosine, sine)


def finish_kernel(
    flag_ref, x_ref, gain_ref, w_ref, cos_ref, sin_ref, mid_ref, qraw_ref, far_ref, nk_ref, nv_ref,
    tokens_ref, gain_grad_ref, raw_ref,
):
    kw = nk_ref.shape[1]
    members = w_ref.shape[0]
    prompt = flag_ref[0] == 1
    far = far_ref[...].astype(F32)
    key_sum = jnp.where(prompt, far[:, :kw], nk_ref[...])
    value_raw = jnp.where(prompt, far[:, kw:], nv_ref[...]).astype(BF16)
    key_raw = turn(key_sum.T, cos_ref[...], sin_ref[...], -1.0).T.astype(BF16)
    query_raw = qraw_ref[...]
    ks = kw // members
    qs = query_raw.shape[1] // members
    normed_grad = None
    for member in range(members):
        raw = jnp.concatenate(
            [
                key_raw[:, member * ks : (member + 1) * ks],
                value_raw[:, member * ks : (member + 1) * ks],
                query_raw[:, member * qs : (member + 1) * qs],
            ],
            axis=1,
        )
        raw_ref[member] = raw
        part = dot_nt(raw, w_ref[member])
        normed_grad = part if normed_grad is None else normed_grad + part
    x = x_ref[...].astype(F32)
    width = x.shape[1]
    inverse = lax.rsqrt(jnp.mean(x * x, axis=-1, keepdims=True) + EPSILON)
    scaled = normed_grad * gain_ref[...].astype(F32)
    inner = jnp.sum(scaled * x, axis=-1, keepdims=True)
    rows_grad = scaled * inverse - x * (inverse**3 * inner / width)
    tokens_ref[...] = (mid_ref[...] + rows_grad).astype(BF16)

    @pl.when(pl.program_id(0) == 0)
    def _():
        gain_grad_ref[...] = jnp.zeros_like(gain_grad_ref)

    gain_grad_ref[...] += jnp.sum(normed_grad * x * inverse, axis=0, keepdims=True)


def finish(flag, x, gain, w, cosine, sine, middle_grad, query_raw, far, near_k, near_v):
    rows, width = x.shape
    kw = near_k.shape[1]
    band = pl.BlockSpec((ROWS, width), lambda i, f: (i, 0))
    row = pl.BlockSpec((1, width), lambda i, f: (0, 0))
    table = pl.BlockSpec((HEAD_SIZE // 2, ROWS), lambda i, f: (0, i))
    thin = pl.BlockSpec((ROWS, kw), lambda i, f: (i, 0))
    return pl.pallas_call(
        finish_kernel,
        out_shape=(
            jax.ShapeDtypeStruct((rows, width), BF16),
            jax.ShapeDtypeStruct((1, width), F32),
            jax.ShapeDtypeStruct((w.shape[0], rows, w.shape[2]), BF16),
        ),
        grid_spec=pltpu.PrefetchScalarGridSpec(
            num_scalar_prefetch=1,
            grid=(rows // ROWS,),
            in_specs=[
                band,
                row,
                pl.BlockSpec(w.shape, lambda i, f: (0, 0, 0), pipeline_mode=pl.Buffered(1)),
                table,
                table,
                band,
                pl.BlockSpec((ROWS, query_raw.shape[1]), lambda i, f: (i, 0)),
                pl.BlockSpec((ROWS, 2 * kw), lambda i, f: (i, 0)),
                thin,
                thin,
            ],
            out_specs=[
                band,
                row,
                pl.BlockSpec((w.shape[0], ROWS, w.shape[2]), lambda i, f: (0, i, 0)),
            ],
        ),
        compiler_params=params(dimension_semantics=("arbitrary",)),
        name="finish",
    )(flag, x, gain, w, cosine, sine, middle_grad, query_raw, far, near_k, near_v)


def spread_down(value, axis):
    size = lax.axis_size(axis)
    index = lax.axis_index(axis)
    bit = size // 2
    while bit >= 1:
        pairs = [(i, i + bit) for i in range(0, size, 2 * bit)]
        received = lax.ppermute(value, axis, pairs)
        value = jnp.where(index % (2 * bit) == bit, received, value)
        bit //= 2
    return value


def sum_up(value, axis):
    size = lax.axis_size(axis)
    bit = 1
    while bit < size:
        pairs = [(i + bit, i) for i in range(0, size, 2 * bit)]
        received = lax.ppermute(value, axis, pairs)
        value = (value.astype(F32) + received.astype(F32)).astype(value.dtype)
        bit *= 2
    return value


def assemble(piece, groups, members):
    height, width = piece.shape[1:]
    return (
        piece.reshape(groups, members, height, width)
        .transpose(0, 2, 1, 3)
        .reshape(groups * height, members * width)
    )


def swap(value, axis, bit):
    pairs = [(i, i ^ bit) for i in range(lax.axis_size(axis))]
    return lax.ppermute(value, axis, pairs)


def bits_of(axis):
    return [1 << i for i in range(lax.axis_size(axis).bit_length() - 1)]


def relative_columns(right):
    members = lax.axis_size("mem")
    width = right.shape[1] // members
    own = lax.axis_index("mem")
    order = sorted(range(members), key=lambda p: [(p & bit) != 0 for bit in bits_of("mem")])
    return [lax.dynamic_slice_in_dim(right, (own ^ p) * width, width, axis=1) for p in order]


def products(left, blocks):
    groups = lax.axis_size("grp")
    half = len(blocks) // 2
    halves = []
    for part in (blocks[:half], blocks[half:]):
        term = dot_tn(left, jnp.concatenate(part, axis=1)).astype(BF16)
        halves.append(term.reshape(groups, -1, term.shape[1]))
    return halves


def reduce_terms(halves, order):
    keep, send = halves
    first = bits_of("mem")[0]
    value = keep.astype(F32) + swap(send, "mem", first).astype(F32)
    left = bits_of("grp")[::-1]
    for axis, bit in order:
        value = value.astype(BF16)
        if axis == "mem":
            half = value.shape[2] // 2
            keep, send = value[:, :, :half], value[:, :, half:]
        else:
            place = left.index(bit)
            left = left[:place] + left[place + 1 :]
            shape = value.shape
            value = value.reshape(2**place, 2, -1, shape[1], shape[2])
            side = (lax.axis_index("grp") // bit) % 2
            keep, send = (
                lax.dynamic_index_in_dim(value, which, 1, keepdims=False).reshape(
                    -1, shape[1], shape[2]
                )
                for which in (side, 1 - side)
            )
        value = keep.astype(F32) + swap(send, axis, bit).astype(F32)
    return value[0]


def gather(shard):
    return lax.all_gather(shard[None], ("grp", "mem"), axis=0, tiled=True)


def orders():
    mem = [("mem", bit) for bit in bits_of("mem")[1:]]
    grp = [("grp", bit) for bit in bits_of("grp")]
    return mem + grp, grp + mem, grp[1:] + mem + grp[:1]


def body(
    tokens, attn_gain, mlp_gain, query_weight, key_matrix, value_matrix, output_weight,
    gate_weight, up_weight, down_weight, cotangent,
):
    groups = lax.axis_size("grp")
    members = lax.axis_size("mem")
    qs = query_weight.shape[1]
    ks = key_matrix.shape[1]
    fs = gate_weight.shape[1]
    height = query_weight.shape[0]
    narrow = 2 * ks + qs
    gains = jnp.pad(jnp.stack([attn_gain, mlp_gain]), ((0, 6), (0, narrow - attn_gain.shape[0])))
    first = jnp.concatenate(
        [jnp.concatenate([key_matrix, value_matrix, query_weight], axis=1), gains], axis=0
    )
    first = jnp.concatenate([first, jnp.pad(output_weight, ((0, 8), (0, 0)))], axis=1)
    first = gather(first)
    second = first[:, :height, narrow:]
    third = gather(jnp.concatenate([gate_weight, up_weight], axis=1))
    down_weight, third = lax.optimization_barrier((down_weight, third))
    fourth = gather(down_weight)
    gain_rows = first[:members, height : height + 2, : attn_gain.shape[0]]
    gain_one = gain_rows[:, 0].reshape(1, -1)
    gain_two = gain_rows[:, 1].reshape(1, -1)
    w_qkv = (
        first[:, :height, :narrow]
        .reshape(groups, members, height, narrow)
        .transpose(1, 0, 2, 3)
        .reshape(members, groups * height, narrow)
    )
    prompt_flag = lax.axis_index("mem") == 0
    flag = prompt_flag.astype(jnp.int32).reshape(1)
    x = tokens[0]
    rows = x.shape[0]
    local = jnp.arange(rows)
    positions = jnp.where(prompt_flag, local, rows + local % CONT_LEN).astype(F32)
    half = HEAD_SIZE // 2
    freq = 10000.0 ** (-jnp.arange(half, dtype=F32) * 2.0 / HEAD_SIZE)
    angle = freq[:, None] * positions[None, :]
    cosine, sine = jnp.cos(angle), jnp.sin(angle)
    normed, q_t, k, v = project(x, gain_one, w_qkv, cosine, sine)
    kw = k.shape[1]
    common = spread_down(jnp.concatenate([k, v], axis=1), "mem")
    pk, pv = common[:, :kw], common[:, kw:]
    mixed, lse = attention_forward(flag, q_t, k, v, pk, pv)
    w_out = assemble(second, groups, members)
    w_gate = assemble(third[:, :, :fs], groups, members)
    w_up = assemble(third[:, :, fs:], groups, members)
    w_down = assemble(fourth, groups, members)
    middle = x.astype(F32) + dot_nn(mixed, w_out)
    inverse_two = lax.rsqrt(jnp.mean(middle * middle, axis=-1, keepdims=True) + EPSILON)
    gain_two = gain_two.astype(F32)
    normed_two = (middle * inverse_two * gain_two).astype(BF16)
    gate = dot_nn(normed_two, w_gate)
    up = dot_nn(normed_two, w_up)
    sigma = jax.nn.sigmoid(gate)
    hidden = (gate * sigma * up).astype(BF16)
    output = (middle + dot_nn(hidden, w_down)).astype(BF16)[None]
    upstream = cotangent[0]
    order_a, order_b, order_c = orders()
    down_terms = products(hidden, relative_columns(upstream))
    hidden_grad = dot_nt(upstream, w_down)
    gate_grad = (hidden_grad * up * sigma * (1.0 + gate * (1.0 - sigma))).astype(BF16)
    up_grad = (hidden_grad * gate * sigma).astype(BF16)
    gate_terms = products(normed_two, relative_columns(gate_grad))
    up_terms = products(normed_two, relative_columns(up_grad))
    normed_two_grad = dot_nt(gate_grad, w_gate) + dot_nt(up_grad, w_up)
    scaled = normed_two_grad * gain_two
    mlp_gain_grad = jnp.sum(normed_two_grad * middle * inverse_two, axis=0)
    inner = jnp.sum(scaled * middle, axis=-1, keepdims=True)
    middle_grad = (
        upstream.astype(F32)
        + scaled * inverse_two
        - middle * (inverse_two**3 * inner / middle.shape[-1])
    )
    middle_low = middle_grad.astype(BF16)
    mixed_grad = dot_nt(middle_low, w_out).astype(BF16)
    out_terms = products(mixed, relative_columns(middle_low))
    mixed_grad, down_terms, gate_terms, up_terms, out_terms = lax.optimization_barrier(
        (mixed_grad, down_terms, gate_terms, up_terms, out_terms)
    )
    gate_sum = reduce_terms(gate_terms, order_a)
    up_sum = reduce_terms(up_terms, order_b)
    down_sum = reduce_terms(down_terms, order_c)
    out_sum = reduce_terms(out_terms, order_a)
    query_raw, far_k, far_v, near_k, near_v = attention_backward(
        flag, q_t, k, v, pk, pv, lse, mixed_grad, mixed, cosine, sine
    )
    far = sum_up(jnp.concatenate([far_k, far_v], axis=1).astype(BF16), "mem")
    tokens_grad, attn_gain_grad, raw = finish(
        flag, x, gain_one, w_qkv, cosine, sine, middle_grad, query_raw, far, near_k, near_v
    )
    own = lax.axis_index("mem")
    order = sorted(range(members), key=lambda p: [(p & bit) != 0 for bit in bits_of("mem")])
    blocks = [lax.dynamic_index_in_dim(raw, own ^ p, 0, keepdims=False) for p in order]
    qkv_sum = reduce_terms(products(normed, blocks), order_b)
    gs = attn_gain.shape[0]
    gain_sum = lax.psum(jnp.stack([attn_gain_grad[0], mlp_gain_grad]), ("grp", "mem"))
    gain_sum = lax.dynamic_slice_in_dim(gain_sum, own * gs, gs, axis=1)
    return (
        output,
        tokens_grad[None],
        gain_sum[0],
        gain_sum[1],
        qkv_sum[:, 2 * ks :],
        qkv_sum[:, :ks],
        qkv_sum[:, ks : 2 * ks],
        out_sum,
        gate_sum,
        up_sum,
        down_sum,
    )


def solution(mesh):
    rows = P("grp", "mem", None)
    both = P("grp", "mem")
    gain = P("mem")
    return jax.shard_map(
        body,
        mesh=mesh,
        in_specs=(rows, gain, gain) + (both,) * 7 + (rows,),
        out_specs=(rows, rows, gain, gain) + (both,) * 7,
        check_vma=False,
    )
```
